32 devices in a mesh: groups: 2 (over y), ctx: 4 (over z), chan: 4 (over x, core).
Axes of the slice: x: 2, y: 2, z: 4, core: 2. Of those that a mesh axis runs over, the one named last changes fastest.
Arguments:
- projected: bfloat16 [3, 2048, 4096], P(None, ('groups', 'ctx'), 'chan'), parts along dimension 1, may hold values from -6 to 6
- short_filter: float32 [3, 3, 4096], P(None, None, 'chan'), may hold values from -3 to 3
- decay_rates: float32 [16, 4096], P(None, 'chan'), may hold values from 0.0001953125 to 0.05
- residues: float32 [16, 4096], P(None, 'chan'), may hold values from -1.5 to 1.5
- skip_gain: float32 [4096], P('chan'), may hold values from -4 to 4
- out_weight: bfloat16 [4096, 2048], P('chan'), may hold values from -0.09375 to 0.09375
Outputs:
- layer_out: bfloat16 [2048, 2048], P(('groups', 'ctx'), 'chan'), parts along dimension 0
The draws below stay inside these ranges and needn't reach their ends.
There are 2 independent parts, one for each index of `groups`. The reference program is written for one: setup_inputs(seed, part) draws one part's arguments, and reference() takes and returns one part's arrays. A program takes and returns all parts, laid end to end along the dimension named above; an argument that names none is the same for every part. Nothing has to cross between parts.
All inputs are finite; a program needn't handle non-finite values.
Results may differ from the reference program's by a relative error of at most 0.012.
Values may be sent and summed in bfloat16 or wider, within the bound.
No kernel may reach another device: no remote copies, remote signals or barrier semaphores. Data moves between devices by JAX's collectives and lax.ppermute only.
A program may use at most 128 MiB of HBM per device.

```python
import math
import jax
import jax.numpy as jnp

WIDTH = 4096
OUTW = 2048
MODES = 16
SEQ = 1024


def level_of(key, dims, pieces, low, high):
    factor_of, own = 1.0, jax.random.fold_in(key, 6)
    for dim, shards_of in pieces:
        steps = jnp.exp(jax.random.uniform(jax.random.fold_in(own, dim), (shards_of,), jnp.float32, low / len(pieces), high / len(pieces)))
        factor_of = factor_of * jnp.repeat(steps, dims[dim] // shards_of).reshape([-1 if axis == dim else 1 for axis in range(len(dims))])
    return factor_of


def gaussian(key, shape, width, bound, shards=(), kind=jnp.bfloat16):
    gain = level_of(key, shape, shards, -0.22, 0.18) if shards else 1.0
    entries = jax.random.normal(key, shape, jnp.float32) * width * gain
    return jnp.minimum(jnp.maximum(entries, -bound), bound).astype(kind)


def setup_inputs(seed: int = 0, part: int = 0) -> dict:
    key_of = jax.random.split(jax.random.key(seed), 7)
    part_splits = jax.random.split(jax.random.fold_in(key_of[6], part), 7)
    projected = gaussian(part_splits[0], (3, SEQ, WIDTH), 1.0, 6.0, ((1, 4), (2, 4)))
    short_filter = gaussian(key_of[1], (3, 3, WIDTH), 0.6, 3.0, ((2, 4),), jnp.float32)
    decay_rates = jnp.clip(jnp.exp(math.log(0.05) - 5.5451774 * jax.random.uniform(key_of[2], (MODES, WIDTH), jnp.float32) ** level_of(key_of[2], (MODES, WIDTH), ((1, 4),), -0.2, 0.2)), 0.0001953125, 0.05)
    residues = gaussian(key_of[3], (MODES, WIDTH), 0.25, 1.5, ((1, 4),), jnp.float32)
    skip_gain = gaussian(key_of[4], (WIDTH,), 1.0, 4.0, ((0, 4),), jnp.float32)
    out_weight = gaussian(key_of[5], (WIDTH, OUTW), WIDTH ** -0.5, 0.09375, ((0, 4),))
    return {"projected": projected, "short_filter": short_filter, "decay_rates": decay_rates, "residues": residues, "skip_gain": skip_gain, "out_weight": out_weight}


def reference(projected, short_filter, decay_rates, residues, skip_gain, out_weight):
    values = projected.astype(jnp.float32)
    padded = jnp.pad(values, ((0, 0), (2, 0), (0, 0)))
    mixed = short_filter[:, 0, None, :] * padded[:, 2:, :]
    mixed = mixed + short_filter[:, 1, None, :] * padded[:, 1:-1, :]
    mixed = mixed + short_filter[:, 2, None, :] * padded[:, :-2, :]
    query = mixed[0]
    gated = (mixed[1] * mixed[2]).astype(jnp.bfloat16)
    gated_f = gated.astype(jnp.float32)
    scaled = residues * jnp.sqrt(-jnp.expm1(-2.0 * decay_rates))
    times = jnp.arange(SEQ, dtype=jnp.float32)
    filt = jnp.zeros((SEQ, WIDTH), jnp.float32)
    for mode in range(MODES):
        filt = filt + scaled[mode][None, :] * jnp.exp(-decay_rates[mode][None, :] * times[:, None])
    spectrum = jnp.fft.rfft(gated_f, n=2 * SEQ, axis=0) * jnp.fft.rfft(filt, n=2 * SEQ, axis=0)
    conv = jnp.fft.irfft(spectrum, n=2 * SEQ, axis=0)[:SEQ].astype(jnp.float32)
    mixed_out = (query * (conv + skip_gain[None, :] * gated_f)).astype(jnp.bfloat16)
    return jnp.dot(mixed_out, out_weight, preferred_element_type=jnp.float32).astype(jnp.bfloat16)
```

```python
import functools

import jax
import jax.numpy as jnp
from jax import lax
from jax.experimental import pallas as pl
from jax.experimental.pallas import tpu as pltpu
from jax.sharding import PartitionSpec as P

F32 = jnp.float32
BF16 = jnp.bfloat16
LANES = 128
SUB = 8
LAST, FIRST, ROWS = 16, 22, 26


def spread(rows_ref, value):
    rows, width = value.shape
    groups = width // LANES
    for top in range(0, rows, SUB):
        high = min(SUB, rows - top)
        for group in range(groups):
            start = (top // SUB * groups + group) * SUB
            rows_ref[start : start + high, :] = value[top : top + high, group * LANES : (group + 1) * LANES]


def row(rows_ref, index, groups):
    start = index // SUB * (groups * SUB) + index % SUB
    return rows_ref[pl.ds(start, groups, stride=SUB), :]


def tap(flt, comp, now, back1, back2):
    return flt[3 * comp] * now + flt[3 * comp + 1] * back1 + flt[3 * comp + 2] * back2


def state_kernel(key_ref, value_ref, tail_ref, filter_ref, decay_ref, gated_ref, wire_ref, state_ref, lam_ref, mul_ref, flt_ref,
                 key_rows, value_rows, small_rows, back_ref):
    step, steps = pl.program_id(0), pl.num_programs(0)
    block, width = key_ref.shape[1:]
    groups, modes = width // LANES, decay_ref.shape[0]
    spread(key_rows, key_ref[0].astype(F32))
    spread(value_rows, value_ref[0].astype(F32))

    @pl.when(step == 0)
    def _():
        spread(small_rows, decay_ref[...])
        for mode in range(modes):
            lam = row(small_rows, mode, groups)
            lam_ref[mode] = lam
            mul_ref[mode] = jnp.exp(-lam)
        for comp in range(3):
            spread(small_rows, filter_ref[comp])
            for j in range(3):
                flt_ref[3 * comp + j] = row(small_rows, j, groups)
        tail = tail_ref[0].astype(F32)
        spread(small_rows, tail)
        for j in range(2):
            wire_ref[LAST + j] = row(small_rows, tail.shape[0] - 2 + j, groups).astype(BF16)
            wire_ref[FIRST + j] = row(key_rows, j, groups).astype(BF16)
            wire_ref[FIRST + 2 + j] = row(value_rows, j, groups).astype(BF16)
        state_ref[...] = jnp.zeros_like(state_ref)
        back_ref[...] = jnp.zeros_like(back_ref)

    muls = [mul_ref[mode] for mode in range(modes)]
    flt = [flt_ref[j] for j in range(9)]
    opening = jnp.where((step == 0) & (lax.axis_index("ctx") > 0), 0.0, 1.0)

    def eight(th, carry):
        states, key1, key2, value1, value2 = carry
        states = list(states)
        keep = jnp.where(th == 0, opening, 1.0)
        for tl in range(SUB):
            start = th * (groups * SUB) + tl
            key = key_rows[pl.ds(start, groups, stride=SUB), :]
            value = value_rows[pl.ds(start, groups, stride=SUB), :]
            gated = tap(flt, 1, key, key1, key2) * tap(flt, 2, value, value1, value2)
            if tl < 2:
                gated = gated * keep
            gated_ref[th * SUB + tl] = gated
            states = [state * mul + gated for state, mul in zip(states, muls)]
            key1, key2, value1, value2 = key, key1, value, value1
        return tuple(states), key1, key2, value1, value2

    states, key1, key2, value1, value2 = lax.fori_loop(
        0, block // SUB, eight,
        (tuple(state_ref[mode] for mode in range(modes)), back_ref[0], back_ref[1], back_ref[2], back_ref[3]),
    )
    for mode in range(modes):
        state_ref[mode] = states[mode]
    for place, kept in enumerate((key1, key2, value1, value2)):
        back_ref[place] = kept

    @pl.when(step == steps - 1)
    def _():
        for mode in range(modes):
            wire_ref[mode] = states[mode].astype(BF16)
        wire_ref[LAST + 2] = key2.astype(BF16)
        wire_ref[LAST + 3] = key1.astype(BF16)
        wire_ref[LAST + 4] = value2.astype(BF16)
        wire_ref[LAST + 5] = value1.astype(BF16)


def own_states(projected, short_filter, decay_rates, block):
    _, length, width = projected.shape
    groups, modes = width // LANES, decay_rates.shape[0]
    whole = lambda *shape: pl.BlockSpec(shape, lambda i: (0,) * len(shape))
    tail = 2 * SUB
    return pl.pallas_call(
        state_kernel,
        name="own_states",
        grid=(length // block,),
        in_specs=[
            pl.BlockSpec((1, block, width), lambda i: (1, i, 0)),
            pl.BlockSpec((1, block, width), lambda i: (2, i, 0)),
            pl.BlockSpec((1, tail, width), lambda i: (0, length // tail - 1, 0)),
            whole(3, 3, width),
            whole(modes, width),
        ],
        out_specs=[
            pl.BlockSpec((block, groups, LANES), lambda i: (i, 0, 0)),
            whole(ROWS, groups, LANES),
            whole(modes, groups, LANES),
            whole(modes, groups, LANES),
            whole(modes, groups, LANES),
            whole(9, groups, LANES),
        ],
        out_shape=[
            jax.ShapeDtypeStruct((length, groups, LANES), F32),
            jax.ShapeDtypeStruct((ROWS, groups, LANES), BF16),
            jax.ShapeDtypeStruct((modes, groups, LANES), F32),
            jax.ShapeDtypeStruct((modes, groups, LANES), F32),
            jax.ShapeDtypeStruct((modes, groups, LANES), F32),
            jax.ShapeDtypeStruct((9, groups, LANES), F32),
        ],
        scratch_shapes=[
            pltpu.VMEM((block * groups, LANES), F32),
            pltpu.VMEM((block * groups, LANES), F32),
            pltpu.VMEM((modes * groups, LANES), F32),
            pltpu.VMEM((4, groups, LANES), F32),
        ],
        compiler_params=pltpu.CompilerParams(vmem_limit_bytes=16 << 20),
    )(projected, projected, projected, short_filter, decay_rates)


def near_kernel(query_ref, gated_ref, mul_ref, scaled_ref, skip_ref, flt_ref, start_ref, near_ref, mixed_ref, coef_ref, end_ref,
                query_rows, small_rows, back_ref, *, opens):
    step = pl.program_id(0)
    block, width = query_ref.shape[1:]
    groups, modes = width // LANES, scaled_ref.shape[0]
    spread(query_rows, query_ref[0].astype(F32))

    @pl.when(step == 0)
    def _():
        spread(small_rows, scaled_ref[...])
        for mode in range(modes):
            coef_ref[mode] = row(small_rows, mode, groups)
            end_ref[mode] = jnp.zeros_like(end_ref[mode]) if opens else start_ref[mode]
        for j in range(2):
            back_ref[j] = jnp.zeros_like(back_ref[j]) if opens else start_ref[modes + j]

    skip = skip_ref[...]
    flt = [flt_ref[j] for j in range(3)]
    opening = jnp.where(step == 0, 0.0, 1.0) if opens else None

    def eight(th, carry):
        states, query1, query2 = carry
        states = list(states)
        keep = jnp.where(th == 0, opening, 1.0) if opens else None
        for tl in range(SUB):
            query = query_rows[pl.ds(th * (groups * SUB) + tl, groups, stride=SUB), :]
            gated = gated_ref[th * SUB + tl]
            if tl < 2 and opens:
                gated = gated * keep
            total = [skip * gated]
            for mode in range(modes):
                states[mode] = states[mode] * mul_ref[mode] + gated
                total.append(states[mode] * coef_ref[mode])
            while len(total) > 1:
                total = [sum(total[i : i + 2][1:], total[i]) for i in range(0, len(total), 2)]
            near_ref[th * SUB + tl] = total[0]
            mixed_ref[th * SUB + tl] = tap(flt, 0, query, query1, query2)
            query1, query2 = query, query1
        return tuple(states), query1, query2

    states, query1, query2 = lax.fori_loop(
        0, block // SUB, eight, (tuple(end_ref[mode] for mode in range(modes)), back_ref[0], back_ref[1])
    )
    for mode in range(modes):
        end_ref[mode] = states[mode]
    for j, kept in enumerate((query1, query2)):
        back_ref[j] = kept
        end_ref[modes + j] = kept


def near_part(projected, gated, mul, scaled, skip, flt, start, first, count, block):
    _, length, width = projected.shape
    groups, modes = width // LANES, scaled.shape[0]
    whole = lambda *shape: pl.BlockSpec(shape, lambda i: (0,) * len(shape))
    opens = start is None
    offset = first // block
    return pl.pallas_call(
        functools.partial(near_kernel, opens=opens),
        name="near_first" if opens else "near_next",
        grid=(count // block,),
        in_specs=[
            pl.BlockSpec((1, block, width), lambda i: (0, i + offset, 0)),
            pl.BlockSpec((block, groups, LANES), lambda i: (i + offset, 0, 0)),
            whole(modes, groups, LANES),
            whole(modes, width),
            whole(groups, LANES),
            whole(9, groups, LANES),
            whole(*(mul if opens else start).shape),
        ],
        out_specs=[
            pl.BlockSpec((block, groups, LANES), lambda i: (i, 0, 0)),
            pl.BlockSpec((block, groups, LANES), lambda i: (i, 0, 0)),
            whole(modes, groups, LANES),
            whole(modes + 2, groups, LANES),
        ],
        out_shape=[
            jax.ShapeDtypeStruct((count, groups, LANES), F32),
            jax.ShapeDtypeStruct((count, groups, LANES), F32),
            jax.ShapeDtypeStruct((modes, groups, LANES), F32),
            jax.ShapeDtypeStruct((modes + 2, groups, LANES), F32),
        ],
        scratch_shapes=[
            pltpu.VMEM((block * groups, LANES), F32),
            pltpu.VMEM((modes * groups, LANES), F32),
            pltpu.VMEM((2, groups, LANES), F32),
        ],
        compiler_params=pltpu.CompilerParams(vmem_limit_bytes=16 << 20),
    )(projected, gated, mul, scaled, skip, flt, mul if opens else start)


def opening_pair(flt, first, last):
    pair = []
    for t in range(2):
        mixed = []
        for c in range(2):
            now = first[c][t]
            back1 = first[c][0] if t else last[c][1]
            back2 = last[c][1] if t else last[c][0]
            mixed.append(tap(flt, c + 1, now, back1, back2))
        pair.append(mixed[0] * mixed[1])
    return pair


def join_kernel(state_ref, own_ref, got_ref, lam_ref, flt_ref, out_ref, agg_ref, *, level, tokens):
    modes = lam_ref.shape[0]
    later = (lax.axis_index("ctx") >> level) & 1
    own = lambda r: own_ref[r].astype(F32)
    got = lambda r: got_ref[r].astype(F32)
    is_later = jnp.broadcast_to(later, out_ref.shape[1:]) == 1
    ahead = lambda r: jnp.where(is_later, got(r), own(r))
    after = lambda r: jnp.where(is_later, own(r), got(r))
    flt = [flt_ref[j] for j in range(9)]
    first = [[after(FIRST + 2 * c + t) for t in range(2)] for c in range(2)]
    last = [[ahead(LAST + 2 + 2 * c + t) for t in range(2)] for c in range(2)]
    pair = opening_pair(flt, first, last)
    for mode in range(modes):
        lam = lam_ref[mode]
        mine, theirs = state_ref[mode], got(mode)
        front, back = jnp.where(is_later, theirs, mine), jnp.where(is_later, mine, theirs)
        joined = back + jnp.exp(-lam * tokens) * front
        joined = joined + jnp.exp(-lam * (tokens - 1)) * pair[0] + jnp.exp(-lam * (tokens - 2)) * pair[1]
        out_ref[mode] = joined.astype(BF16)
        agg_ref[mode] = joined
    for r in range(LAST, FIRST):
        out_ref[r] = after(r).astype(BF16)
    for r in range(FIRST, out_ref.shape[0]):
        out_ref[r] = ahead(r).astype(BF16)


def join(states, own, got, lam, flt, level, tokens, rows):
    modes, groups, _ = lam.shape
    return pl.pallas_call(
        functools.partial(join_kernel, level=level, tokens=tokens),
        name="join_runs",
        out_shape=[
            jax.ShapeDtypeStruct((rows, groups, LANES), BF16),
            jax.ShapeDtypeStruct((modes, groups, LANES), F32),
        ],
        compiler_params=pltpu.CompilerParams(vmem_limit_bytes=8 << 20),
    )(states, own, got, lam, flt)


def columns_copy(weight_ref, held_ref, sem, mine, relative, place):
    wide = held_ref.shape[-1]
    start = pl.multiple_of((mine ^ relative) * wide, LANES)
    return pltpu.make_async_copy(weight_ref.at[:, pl.ds(start, wide)], held_ref.at[place], sem.at[place])


def far_kernel(*refs, levels, splits, tokens):
    got = refs[:levels]
    nears, queries = refs[levels : levels + splits], refs[levels + splits : levels + 2 * splits]
    (head_ref, mul_ref, coef_ref, lam_ref, skip_ref, flt_ref, weight_ref, mixed_out_ref, part_ref,
     decayed_ref, small_rows, out_rows, held_ref, sem) = refs[levels + 2 * splits :]
    modes, groups, _ = lam_ref.shape
    length, width = mixed_out_ref.shape
    halves = held_ref.shape[0]
    mine, place = lax.axis_index("chan"), lax.axis_index("ctx")
    for r in range(halves):
        columns_copy(weight_ref, held_ref, sem, mine, 2 * r + 1, r).start()

    flt = [flt_ref[j] for j in range(9)]
    skip = skip_ref[...]
    lams = [lam_ref[mode] for mode in range(modes)]
    states = [jnp.zeros((groups, LANES), F32)] * modes
    last = [jnp.zeros((groups, LANES), F32)] * 6
    first = [jnp.zeros((groups, LANES), F32)] * 4
    for level in range(levels):
        here = (place >> level) & 1
        held = place & ((1 << level) - 1)
        taken = jnp.broadcast_to(here, (groups, LANES)) == 1
        filled = jnp.broadcast_to(held, (groups, LANES)) > 0
        wire = [got[level][r].astype(F32) for r in range(got[level].shape[0])]
        if level:
            pair = opening_pair(
                flt,
                [[first[2 * c + t] for t in range(2)] for c in range(2)],
                [[wire[LAST + 2 + 2 * c + t] for t in range(2)] for c in range(2)],
            )
            span = (held * tokens).astype(F32)
            for mode in range(modes):
                joined = states[mode] + jnp.exp(-lams[mode] * span) * wire[mode]
                more = jnp.exp(-lams[mode] * (span - 1)) * pair[0] + jnp.exp(-lams[mode] * (span - 2)) * pair[1]
                joined = joined + jnp.where(filled, more, 0.0)
                states[mode] = jnp.where(taken, joined, states[mode])
            last = [jnp.where(taken & ~filled, wire[LAST + j], last[j]) for j in range(6)]
        else:
            states = [jnp.where(taken, wire[mode], states[mode]) for mode in range(modes)]
            last = [jnp.where(taken, wire[LAST + j], last[j]) for j in range(6)]
        if level < levels - 1:
            first = [jnp.where(taken, wire[FIRST + j], first[j]) for j in range(4)]

    head = []
    for comp in range(3):
        spread(small_rows, head_ref[comp].astype(F32))
        head.append([row(small_rows, t, groups) for t in range(2)])
    pair = opening_pair(flt, head[1:], [[last[2 + 2 * c + t] for t in range(2)] for c in range(2)])
    asked = [
        tap(flt, 0, head[0][0], last[1], last[0]),
        tap(flt, 0, head[0][1], head[0][0], last[1]),
    ]
    openers = [skip * pair[0], skip * pair[1]]
    for mode in range(modes):
        mul, coef = mul_ref[mode], coef_ref[mode]
        zero = states[mode] * mul + pair[0]
        one = zero * mul + pair[1]
        openers = [openers[0] + coef * zero, openers[1] + coef * one]
        decayed_ref[mode] = coef * (one * jnp.exp(2.0 * lams[mode]))

    total = tuple(decayed_ref[mode] for mode in range(modes))
    count = length // splits
    for s in range(splits):
        near_ref, query_ref = nears[s], queries[s]

        def eight(th, carry):
            waves = list(carry)
            for tl in range(SUB):
                waves = [wave * mul_ref[mode] for mode, wave in enumerate(waves)]
                terms = [near_ref[th * SUB + tl]] + waves
                while len(terms) > 1:
                    terms = [sum(terms[i : i + 2][1:], terms[i]) for i in range(0, len(terms), 2)]
                start = (th + s * count // SUB) * (groups * SUB) + tl
                out_rows[pl.ds(start, groups, stride=SUB), :] = terms[0] * query_ref[th * SUB + tl]
            return tuple(waves)

        total = lax.fori_loop(0, count // SUB, eight, total)
    for t in range(2):
        out_rows[pl.ds(t, groups, stride=SUB), :] = openers[t] * asked[t]

    def gather(pair_of, _):
        for group in range(groups):
            tiles = [out_rows[pl.ds(((pair_of * 2 + h) * groups + group) * SUB, SUB), :] for h in range(2)]
            rows = pl.ds(pl.multiple_of(pair_of * 2 * SUB, 2 * SUB), 2 * SUB)
            mixed_out_ref[rows, group * LANES : (group + 1) * LANES] = jnp.concatenate(tiles, axis=0).astype(BF16)
        return 0

    lax.fori_loop(0, length // (2 * SUB), gather, 0)
    for r in range(halves):
        columns_copy(weight_ref, held_ref, sem, mine, 2 * r + 1, r).wait()
        part_ref[r] = jnp.dot(mixed_out_ref[...], held_ref[r], preferred_element_type=F32).astype(BF16)


def far_part(got, nears, queries, projected, mul, coef, lam, skip, flt, weight):
    _, length, width = projected.shape
    modes, groups, _ = lam.shape
    count = lax.axis_size("chan")
    wide = weight.shape[1] // count
    full = pl.BlockSpec(memory_space=pltpu.VMEM)
    levels, splits = len(got), len(nears)
    head = 2 * SUB
    return pl.pallas_call(
        functools.partial(far_kernel, levels=levels, splits=splits, tokens=length),
        name="far_part",
        grid=(1,),
        in_specs=[full] * (levels + 2 * splits)
        + [pl.BlockSpec((3, head, width), lambda i: (0, 0, 0))]
        + [full] * 5
        + [pl.BlockSpec(memory_space=pl.ANY)],
        out_specs=[full, full],
        out_shape=[
            jax.ShapeDtypeStruct((length, width), BF16),
            jax.ShapeDtypeStruct((count // 2, length, wide), BF16),
        ],
        scratch_shapes=[
            pltpu.VMEM((modes, groups, LANES), F32),
            pltpu.VMEM((head * groups, LANES), F32),
            pltpu.VMEM((length * groups, LANES), F32),
            pltpu.VMEM((count // 2, width, wide), BF16),
            pltpu.SemaphoreType.DMA((count // 2,)),
        ],
        compiler_params=pltpu.CompilerParams(vmem_limit_bytes=24 << 20),
    )(*got, *nears, *queries, projected, mul, coef, lam, skip, flt, weight)


def keep_kernel(mixed_out_ref, weight_ref, kept_ref, held_ref, sem):
    mine = lax.axis_index("chan")
    halves = held_ref.shape[0]
    for r in reversed(range(halves)):
        columns_copy(weight_ref, held_ref, sem, mine, 2 * r, r).start()
    for r in reversed(range(halves)):
        columns_copy(weight_ref, held_ref, sem, mine, 2 * r, r).wait()
        kept_ref[r] = jnp.dot(mixed_out_ref[...], held_ref[r], preferred_element_type=F32)


def kept_part(mixed_out, weight):
    length, width = mixed_out.shape
    count = lax.axis_size("chan")
    wide = weight.shape[1] // count
    full = pl.BlockSpec(memory_space=pltpu.VMEM)
    return pl.pallas_call(
        keep_kernel,
        name="kept_part",
        in_specs=[full, pl.BlockSpec(memory_space=pl.ANY)],
        out_specs=full,
        out_shape=jax.ShapeDtypeStruct((count // 2, length, wide), F32),
        scratch_shapes=[
            pltpu.VMEM((count // 2, width, wide), BF16),
            pltpu.SemaphoreType.DMA((count // 2,)),
        ],
        compiler_params=pltpu.CompilerParams(vmem_limit_bytes=16 << 20),
    )(mixed_out, weight)


def add_kernel(*refs):
    total = refs[0][...].astype(F32)
    for ref in refs[1:-1]:
        total = total + ref[...].astype(F32)
    refs[-1][...] = total.astype(BF16)


def add_blocks(parts, picks, blocks):
    _, length, wide = parts[0].shape
    return pl.pallas_call(
        add_kernel,
        name="add_blocks",
        grid=(blocks,),
        in_specs=[
            pl.BlockSpec((1, length, wide), functools.partial(lambda i, level: (picks(level, i), 0, 0), level=max(0, p - 1)))
            for p in range(len(parts))
        ],
        out_specs=pl.BlockSpec((1, length, wide), lambda i: (i, 0, 0)),
        out_shape=jax.ShapeDtypeStruct((blocks, length, wide), BF16),
        compiler_params=pltpu.CompilerParams(vmem_limit_bytes=8 << 20),
    )(*parts)


def body(projected, short_filter, decay_rates, residues, skip_gain, out_weight):
    _, length, width = projected.shape
    groups = width // LANES
    ctx, chan = lax.axis_size("ctx"), lax.axis_size("chan")
    levels, stages = ctx.bit_length() - 1, chan.bit_length() - 1
    assert ctx == 1 << levels and chan == 1 << stages and levels and stages
    skip = skip_gain.reshape(groups, LANES)
    block = min(64, length // 2)

    scaled = residues * jnp.sqrt(-jnp.expm1(-2.0 * decay_rates))
    gated, wire, states, lam, mul, flt = own_states(projected, short_filter, decay_rates, block)

    got, nears, queries = [], [], []
    coef = end = None
    for level in range(levels):
        if level == levels - 1:
            wire = wire[:FIRST]
        bit = 1 << level
        got.append(lax.ppermute(wire, "ctx", [(i, i ^ bit) for i in range(ctx)]))
        if level < 2:
            near, query, first_coef, end = near_part(
                projected, gated, mul, scaled, skip, flt, end, level * (length // 2), length // 2, block
            )
            coef = first_coef if coef is None else coef
            nears.append(near)
            queries.append(query)
        if level < levels - 1:
            rows = FIRST if level == levels - 2 else ROWS
            wire, states = join(states, wire, got[level], lam, flt, level, length << level, rows)
    while len(nears) < 2:
        near, query, _, end = near_part(projected, gated, mul, scaled, skip, flt, end, length // 2, length // 2, block)
        nears.append(near)
        queries.append(query)

    mixed_out, part = far_part(got, nears, queries, projected, mul, coef, lam, skip, flt, out_weight)
    parts = [None, lax.ppermute(part, "chan", [(i, i ^ 1) for i in range(chan)])]
    parts[0] = kept_part(mixed_out, out_weight)
    for stage in range(1, stages):
        send = add_blocks(
            parts, lambda level, i, stage=stage: ((i << (stage + 1)) | (1 << stage)) >> (level + 1), chan >> (stage + 1)
        )
        parts.append(lax.ppermute(send, "chan", [(i, i ^ (1 << stage)) for i in range(chan)]))
    return add_blocks(parts, lambda level, i: 0, 1)[0]


def solution(mesh):
    in_specs = (
        P(None, ("groups", "ctx"), "chan"),
        P(None, None, "chan"),
        P(None, "chan"),
        P(None, "chan"),
        P("chan"),
        P("chan", None),
    )
    out_specs = P(("groups", "ctx"), "chan")
    return jax.shard_map(body, mesh=mesh, in_specs=in_specs, out_specs=out_specs, check_vma=False)
```

```python
import functools

import jax
import jax.numpy as jnp
from jax import lax
from jax.experimental import pallas as pl
from jax.experimental.pallas import tpu as pltpu
from jax.sharding import PartitionSpec as P

F32 = jnp.float32
BF16 = jnp.bfloat16
LANES = 128
SUB = 8
LAST, FIRST, ROWS = 16, 22, 26


def spread(rows_ref, value):
    rows, width = value.shape
    groups = width // LANES
    for top in range(0, rows, SUB):
        high = min(SUB, rows - top)
        for group in range(groups):
            start = (top // SUB * groups + group) * SUB
            rows_ref[start : start + high, :] = value[top : top + high, group * LANES : (group + 1) * LANES]


def row(rows_ref, index, groups):
    start = index // SUB * (groups * SUB) + index % SUB
    return rows_ref[pl.ds(start, groups, stride=SUB), :]


def tap(flt, comp, now, back1, back2):
    return flt[3 * comp] * now + flt[3 * comp + 1] * back1 + flt[3 * comp + 2] * back2


def state_kernel(projected_ref, filter_ref, decay_ref, residue_ref, skip_ref, gated_ref, wire_ref, state_ref, lam_ref, mul_ref, flt_ref,
                 query_ref, asked_ref, decay_held, residue_held, skip_held,
                 held_ref, filter_held, key_rows, value_rows, small_rows, sems):
    _, length, width = projected_ref.shape
    chunks, block = held_ref.shape[1], held_ref.shape[2]
    groups, modes = width // LANES, decay_ref.shape[0]
    tail = 2 * SUB

    def piece(comp, chunk):
        rows = pl.ds(chunk * block, block)
        return pltpu.make_async_copy(projected_ref.at[1 + comp, rows, :], held_ref.at[comp, chunk], sems.at[comp, chunk])

    extras = [
        pltpu.make_async_copy(decay_ref, decay_held, sems.at[2, 0]),
        pltpu.make_async_copy(filter_ref, filter_held, sems.at[2, 1]),
        pltpu.make_async_copy(projected_ref.at[0], query_ref, sems.at[2, 2]),
        pltpu.make_async_copy(residue_ref, residue_held, sems.at[3, 0]),
        pltpu.make_async_copy(skip_ref, skip_held, sems.at[3, 1]),
    ]
    extras[0].start()
    extras[1].start()
    for chunk in range(chunks):
        for comp in range(2):
            piece(comp, chunk).start()
    for extra in extras[2:]:
        extra.start()
    extras[0].wait()
    spread(small_rows, decay_held[...])
    muls = []
    for mode in range(modes):
        lam = row(small_rows, mode, groups)
        lam_ref[mode] = lam
        muls.append(jnp.exp(-lam))
        mul_ref[mode] = muls[mode]
    extras[1].wait()
    flt = []
    for comp in range(3):
        spread(small_rows, filter_held[comp])
        for j in range(3):
            flt.append(row(small_rows, j, groups))
            flt_ref[3 * comp + j] = flt[-1]
    opening = jnp.where(lax.axis_index("ctx") > 0, 0.0, 1.0)
    zero = jnp.zeros((groups, LANES), F32)

    def whole_chunk(chunk, carry):
        for comp in range(2):
            piece(comp, chunk).wait()
        spread(key_rows, held_ref[0, chunk].astype(F32))
        spread(value_rows, held_ref[1, chunk].astype(F32))

        def eight(th, carry):
            states, key1, key2, value1, value2 = carry
            states = list(states)
            place = chunk * (block // SUB) + th
            keep = jnp.where(place == 0, opening, 1.0)
            for tl in range(SUB):
                start = th * (groups * SUB) + tl
                key = key_rows[pl.ds(start, groups, stride=SUB), :]
                value = value_rows[pl.ds(start, groups, stride=SUB), :]
                gated = tap(flt, 1, key, key1, key2) * tap(flt, 2, value, value1, value2)
                if tl < 2:
                    gated = gated * keep
                gated_ref[place * SUB + tl] = gated
                states = [state * mul + gated for state, mul in zip(states, muls)]
                key1, key2, value1, value2 = key, key1, value, value1
            return tuple(states), key1, key2, value1, value2

        return lax.fori_loop(0, block // SUB, eight, carry)

    states, key1, key2, value1, value2 = lax.fori_loop(0, chunks, whole_chunk, ((zero,) * modes, zero, zero, zero, zero))
    for mode in range(modes):
        state_ref[mode] = states[mode]
        wire_ref[mode] = states[mode].astype(BF16)
    wire_ref[LAST + 2] = key2.astype(BF16)
    wire_ref[LAST + 3] = key1.astype(BF16)
    wire_ref[LAST + 4] = value2.astype(BF16)
    wire_ref[LAST + 5] = value1.astype(BF16)
    for extra in extras[2:]:
        extra.wait()
    spread(small_rows, query_ref[length - tail :].astype(F32))
    for j in range(2):
        wire_ref[LAST + j] = row(small_rows, tail - 2 + j, groups).astype(BF16)
    spread(small_rows, query_ref[:tail].astype(F32))
    for j in range(2):
        asked_ref[j] = row(small_rows, j, groups)
    for comp in range(2):
        spread(small_rows, held_ref[comp, 0][: 2 * SUB].astype(F32))
        for j in range(2):
            wire_ref[FIRST + 2 * comp + j] = row(small_rows, j, groups).astype(BF16)


def own_states(projected, short_filter, decay_rates, residues, skip, block):
    _, length, width = projected.shape
    groups, modes = width // LANES, decay_rates.shape[0]
    chunks = length // block
    return pl.pallas_call(
        state_kernel,
        name="own_states",
        in_specs=[pl.BlockSpec(memory_space=pltpu.HBM)] * 5,
        out_specs=[pl.BlockSpec(memory_space=pltpu.VMEM)] * 11,
        out_shape=[
            jax.ShapeDtypeStruct((length, groups, LANES), F32),
            jax.ShapeDtypeStruct((ROWS, groups, LANES), BF16),
            jax.ShapeDtypeStruct((modes, groups, LANES), F32),
            jax.ShapeDtypeStruct((modes, groups, LANES), F32),
            jax.ShapeDtypeStruct((modes, groups, LANES), F32),
            jax.ShapeDtypeStruct((9, groups, LANES), F32),
            jax.ShapeDtypeStruct((length, width), BF16),
            jax.ShapeDtypeStruct((2, groups, LANES), F32),
            jax.ShapeDtypeStruct((modes, width), F32),
            jax.ShapeDtypeStruct((modes, width), F32),
            jax.ShapeDtypeStruct((groups, LANES), F32),
        ],
        scratch_shapes=[
            pltpu.VMEM((2, chunks, block, width), BF16),
            pltpu.VMEM((3, 3, width), F32),
            pltpu.VMEM((block * groups, LANES), F32),
            pltpu.VMEM((block * groups, LANES), F32),
            pltpu.VMEM((2 * SUB * groups, LANES), F32),
            pltpu.SemaphoreType.DMA((4, max(chunks, 3))),
        ],
        compiler_params=pltpu.CompilerParams(vmem_limit_bytes=16 << 20),
    )(*(pltpu.with_memory_space_constraint(x, pltpu.HBM) for x in (projected, short_filter, decay_rates, residues, skip)))


def near_kernel(query_ref, gated_ref, mul_ref, scaled_ref, skip_ref, flt_ref, start_ref, near_ref, mixed_ref, *rest, opens):
    if opens:
        coef_ref, end_ref, query_rows, small_rows, back_ref = rest
    else:
        end_ref, query_rows, back_ref = rest
        coef_ref = scaled_ref
    step = pl.program_id(0)
    block, width = query_ref.shape
    groups, modes = width // LANES, scaled_ref.shape[0]
    spread(query_rows, query_ref[...].astype(F32))

    @pl.when(step == 0)
    def _():
        if opens:
            spread(small_rows, scaled_ref[...])
        for mode in range(modes):
            if opens:
                coef_ref[mode] = row(small_rows, mode, groups)
            end_ref[mode] = jnp.zeros_like(end_ref[mode]) if opens else start_ref[mode]
        for j in range(2):
            back_ref[j] = jnp.zeros_like(back_ref[j]) if opens else start_ref[modes + j]

    skip = skip_ref[...]
    flt = [flt_ref[j] for j in range(3)]
    opening = jnp.where(step == 0, 0.0, 1.0) if opens else None

    def eight(th, carry):
        states, query1, query2 = carry
        states = list(states)
        keep = jnp.where(th == 0, opening, 1.0) if opens else None
        for tl in range(SUB):
            query = query_rows[pl.ds(th * (groups * SUB) + tl, groups, stride=SUB), :]
            gated = gated_ref[th * SUB + tl]
            if tl < 2 and opens:
                gated = gated * keep
            total = [skip * gated]
            for mode in range(modes):
                states[mode] = states[mode] * mul_ref[mode] + gated
                total.append(states[mode] * coef_ref[mode])
            while len(total) > 1:
                total = [sum(total[i : i + 2][1:], total[i]) for i in range(0, len(total), 2)]
            near_ref[th * SUB + tl] = total[0]
            mixed_ref[th * SUB + tl] = tap(flt, 0, query, query1, query2)
            query1, query2 = query, query1
        return tuple(states), query1, query2

    states, query1, query2 = lax.fori_loop(
        0, block // SUB, eight, (tuple(end_ref[mode] for mode in range(modes)), back_ref[0], back_ref[1])
    )
    for mode in range(modes):
        end_ref[mode] = states[mode]
    for j, kept in enumerate((query1, query2)):
        back_ref[j] = kept
        end_ref[modes + j] = kept


def near_part(asking, gated, mul, scaled, skip, flt, start, first, count, block):
    _, width = asking.shape
    modes, groups, _ = mul.shape
    whole = lambda *shape: pl.BlockSpec(shape, lambda i: (0,) * len(shape))
    opens = start is None
    offset = first // block
    tokens = pl.BlockSpec((block, groups, LANES), lambda i: (i, 0, 0))
    carried = (modes + 2, groups, LANES)
    rows = pltpu.VMEM((block * groups, LANES), F32)
    return pl.pallas_call(
        functools.partial(near_kernel, opens=opens),
        name="near_first" if opens else "near_next",
        grid=(count // block,),
        in_specs=[
            pl.BlockSpec((block, width), lambda i: (i + offset, 0)),
            pl.BlockSpec((block, groups, LANES), lambda i: (i + offset, 0, 0)),
            whole(modes, groups, LANES),
            whole(*scaled.shape),
            whole(groups, LANES),
            whole(9, groups, LANES),
            whole(*(mul if opens else start).shape),
        ],
        out_specs=[tokens, tokens] + ([whole(modes, groups, LANES), whole(*carried)] if opens else []),
        out_shape=[jax.ShapeDtypeStruct((count, groups, LANES), F32)] * 2
        + ([jax.ShapeDtypeStruct(mul.shape, F32), jax.ShapeDtypeStruct(carried, F32)] if opens else []),
        scratch_shapes=([] if opens else [pltpu.VMEM(carried, F32)])
        + [rows]
        + ([pltpu.VMEM((modes * groups, LANES), F32)] if opens else [])
        + [pltpu.VMEM((2, groups, LANES), F32)],
        compiler_params=pltpu.CompilerParams(vmem_limit_bytes=16 << 20),
    )(asking, gated, mul, scaled, skip, flt, mul if opens else start)


def opening_pair(flt, first, last):
    pair = []
    for t in range(2):
        mixed = []
        for c in range(2):
            now = first[c][t]
            back1 = first[c][0] if t else last[c][1]
            back2 = last[c][1] if t else last[c][0]
            mixed.append(tap(flt, c + 1, now, back1, back2))
        pair.append(mixed[0] * mixed[1])
    return pair


def join_kernel(state_ref, own_ref, got_ref, lam_ref, flt_ref, after_ref, out_ref, *aggs, level, tokens):
    modes = lam_ref.shape[0]
    later = (lax.axis_index("ctx") >> level) & 1
    own = lambda r: own_ref[r].astype(F32)
    got = lambda r: got_ref[r].astype(F32)
    is_later = jnp.broadcast_to(later, out_ref.shape[1:]) == 1
    ahead = lambda r: jnp.where(is_later, got(r), own(r))
    after = lambda r: jnp.where(is_later, own(r), got(r))
    flt = [flt_ref[j] for j in range(9)]
    first = [[after(FIRST + 2 * c + t) for t in range(2)] for c in range(2)]
    last = [[ahead(LAST + 2 + 2 * c + t) for t in range(2)] for c in range(2)]
    pair = opening_pair(flt, first, last)
    for mode in range(modes):
        lam = lam_ref[mode]
        mine, theirs = state_ref[mode], got(mode)
        front, back = jnp.where(is_later, theirs, mine), jnp.where(is_later, mine, theirs)
        joined = back + jnp.exp(-lam * tokens) * front
        joined = joined + jnp.exp(-lam * (tokens - 1)) * pair[0] + jnp.exp(-lam * (tokens - 2)) * pair[1]
        out_ref[mode] = joined.astype(BF16)
        for agg_ref in aggs:
            agg_ref[mode] = joined
    for r in range(LAST, FIRST):
        out_ref[r] = after(r).astype(BF16)
    for r in range(FIRST, out_ref.shape[0]):
        out_ref[r] = ahead(r).astype(BF16)


def join(states, own, got, lam, flt, behind, level, tokens, rows, final):
    modes, groups, _ = lam.shape
    return pl.pallas_call(
        functools.partial(join_kernel, level=level, tokens=tokens),
        name="join_runs",
        in_specs=[pl.BlockSpec(memory_space=pltpu.VMEM)] * 5 + [pl.BlockSpec(memory_space=pl.ANY)],
        out_shape=[jax.ShapeDtypeStruct((rows, groups, LANES), BF16)]
        + ([] if final else [jax.ShapeDtypeStruct((modes, groups, LANES), F32)]),
        compiler_params=pltpu.CompilerParams(vmem_limit_bytes=8 << 20),
    )(states, own, got, lam, flt, behind)


def columns(weight_ref, mine, relative, count):
    wide = weight_ref.shape[1] // count
    return weight_ref[:, pl.ds(pl.multiple_of((mine ^ relative) * wide, LANES), wide)]


def far_kernel(*refs, levels, splits, tokens):
    got = refs[:levels]
    nears, queries = refs[levels : levels + splits], refs[levels + splits : levels + 2 * splits]
    (own_ref, asked_ref, mul_ref, coef_ref, lam_ref, skip_ref, flt_ref, weight_ref, mixed_out_ref, part_ref,
     decayed_ref, out_rows) = refs[levels + 2 * splits :]
    modes, groups, _ = lam_ref.shape
    length, width = mixed_out_ref.shape
    halves = part_ref.shape[0]
    mine, place = lax.axis_index("chan"), lax.axis_index("ctx")

    flt = [flt_ref[j] for j in range(9)]
    skip = skip_ref[...]
    lams = [lam_ref[mode] for mode in range(modes)]
    states = [jnp.zeros((groups, LANES), F32)] * modes
    last = [jnp.zeros((groups, LANES), F32)] * 6
    first = [jnp.zeros((groups, LANES), F32)] * 4
    for level in range(levels):
        here = (place >> level) & 1
        held = place & ((1 << level) - 1)
        taken = jnp.broadcast_to(here, (groups, LANES)) == 1
        filled = jnp.broadcast_to(held, (groups, LANES)) > 0
        wire = [got[level][r].astype(F32) for r in range(got[level].shape[0])]
        if level:
            pair = opening_pair(
                flt,
                [[first[2 * c + t] for t in range(2)] for c in range(2)],
                [[wire[LAST + 2 + 2 * c + t] for t in range(2)] for c in range(2)],
            )
            span = (held * tokens).astype(F32)
            for mode in range(modes):
                joined = states[mode] + jnp.exp(-lams[mode] * span) * wire[mode]
                more = jnp.exp(-lams[mode] * (span - 1)) * pair[0] + jnp.exp(-lams[mode] * (span - 2)) * pair[1]
                joined = joined + jnp.where(filled, more, 0.0)
                states[mode] = jnp.where(taken, joined, states[mode])
            last = [jnp.where(taken & ~filled, wire[LAST + j], last[j]) for j in range(6)]
        else:
            states = [jnp.where(taken, wire[mode], states[mode]) for mode in range(modes)]
            last = [jnp.where(taken, wire[LAST + j], last[j]) for j in range(6)]
        if level < levels - 1:
            first = [jnp.where(taken, wire[FIRST + j], first[j]) for j in range(4)]

    head = [[asked_ref[t] for t in range(2)]]
    for c in range(2):
        head.append([own_ref[FIRST + 2 * c + t].astype(F32) for t in range(2)])
    pair = opening_pair(flt, head[1:], [[last[2 + 2 * c + t] for t in range(2)] for c in range(2)])
    asked = [
        tap(flt, 0, head[0][0], last[1], last[0]),
        tap(flt, 0, head[0][1], head[0][0], last[1]),
    ]
    openers = [skip * pair[0], skip * pair[1]]
    for mode in range(modes):
        mul, coef = mul_ref[mode], coef_ref[mode]
        zero = states[mode] * mul + pair[0]
        one = zero * mul + pair[1]
        openers = [openers[0] + coef * zero, openers[1] + coef * one]
        decayed_ref[mode] = coef * (one * jnp.exp(2.0 * lams[mode]))

    total = tuple(decayed_ref[mode] for mode in range(modes))
    count = length // splits
    for s in range(splits):
        near_ref, query_ref = nears[s], queries[s]

        def eight(th, carry):
            waves = list(carry)
            for tl in range(SUB):
                waves = [wave * mul_ref[mode] for mode, wave in enumerate(waves)]
                terms = [near_ref[th * SUB + tl]] + waves
                while len(terms) > 1:
                    terms = [sum(terms[i : i + 2][1:], terms[i]) for i in range(0, len(terms), 2)]
                start = (th + s * count // SUB) * (groups * SUB) + tl
                out_rows[pl.ds(start, groups, stride=SUB), :] = terms[0] * query_ref[th * SUB + tl]
            return tuple(waves)

        total = lax.fori_loop(0, count // SUB, eight, total)
    for t in range(2):
        out_rows[pl.ds(t, groups, stride=SUB), :] = openers[t] * asked[t]

    def gather(pair_of, _):
        for group in range(groups):
            tiles = [out_rows[pl.ds(((pair_of * 2 + h) * groups + group) * SUB, SUB), :] for h in range(2)]
            rows = pl.ds(pl.multiple_of(pair_of * 2 * SUB, 2 * SUB), 2 * SUB)
            mixed_out_ref[rows, group * LANES : (group + 1) * LANES] = jnp.concatenate(tiles, axis=0).astype(BF16)
        return 0

    lax.fori_loop(0, length // (2 * SUB), gather, 0)
    for r in range(halves):
        held = columns(weight_ref, mine, 2 * r + 1, 2 * halves)
        part_ref[r] = jnp.dot(mixed_out_ref[...], held, preferred_element_type=F32).astype(BF16)


def far_part(got, nears, queries, own, asked, mul, coef, lam, skip, flt, weight):
    width, length = weight.shape[0], sum(near.shape[0] for near in nears)
    modes, groups, _ = lam.shape
    count = lax.axis_size("chan")
    wide = weight.shape[1] // count
    full = pl.BlockSpec(memory_space=pltpu.VMEM)
    levels, splits = len(got), len(nears)
    return pl.pallas_call(
        functools.partial(far_kernel, levels=levels, splits=splits, tokens=length),
        name="far_part",
        in_specs=[full] * (levels + 2 * splits)
        + [full] * 8,
        out_specs=[full, full],
        out_shape=[
            jax.ShapeDtypeStruct((length, width), BF16),
            jax.ShapeDtypeStruct((count // 2, length, wide), BF16),
        ],
        scratch_shapes=[
            pltpu.VMEM((modes, groups, LANES), F32),
            pltpu.VMEM((length * groups, LANES), F32),
        ],
        compiler_params=pltpu.CompilerParams(vmem_limit_bytes=24 << 20),
    )(*got, *nears, *queries, own, asked, mul, coef, lam, skip, flt, weight)


def keep_kernel(mixed_out_ref, weight_ref, kept_ref):
    mine = lax.axis_index("chan")
    halves = kept_ref.shape[0]
    for r in range(halves):
        held = columns(weight_ref, mine, 2 * r, 2 * halves)
        kept_ref[r] = jnp.dot(mixed_out_ref[...], held, preferred_element_type=F32)


def kept_part(mixed_out, weight):
    length, width = mixed_out.shape
    count = lax.axis_size("chan")
    wide = weight.shape[1] // count
    full = pl.BlockSpec(memory_space=pltpu.VMEM)
    return pl.pallas_call(
        keep_kernel,
        name="kept_part",
        in_specs=[full, full],
        out_specs=full,
        out_shape=jax.ShapeDtypeStruct((count // 2, length, wide), F32),
        compiler_params=pltpu.CompilerParams(vmem_limit_bytes=16 << 20),
    )(mixed_out, weight)


def add_kernel(*refs):
    total = refs[0][...].astype(F32)
    for ref in refs[1:-1]:
        total = total + ref[...].astype(F32)
    refs[-1][...] = total.astype(BF16)


def add_blocks(parts, picks, blocks):
    _, length, wide = parts[0].shape
    return pl.pallas_call(
        add_kernel,
        name="add_blocks",
        grid=(blocks,),
        in_specs=[
            pl.BlockSpec((1, length, wide), functools.partial(lambda i, level: (picks(level, i), 0, 0), level=max(0, p - 1)))
            for p in range(len(parts))
        ],
        out_specs=pl.BlockSpec((1, length, wide), lambda i: (i, 0, 0)),
        out_shape=jax.ShapeDtypeStruct((blocks, length, wide), BF16),
        compiler_params=pltpu.CompilerParams(vmem_limit_bytes=8 << 20),
    )(*parts)


def body(projected, short_filter, decay_rates, residues, skip_gain, out_weight):
    _, length, width = projected.shape
    groups = width // LANES
    ctx, chan = lax.axis_size("ctx"), lax.axis_size("chan")
    levels, stages = ctx.bit_length() - 1, chan.bit_length() - 1
    assert ctx == 1 << levels and chan == 1 << stages and levels and stages
    skip = skip_gain.reshape(groups, LANES)
    block = min(64, length // 2)

    gated, own, state, lam, mul, flt, asking, asked, decays, weights, skip = own_states(
        projected, short_filter, decay_rates, residues, skip, block
    )
    scaled = weights * jnp.sqrt(-jnp.expm1(-2.0 * decays))
    wire, states = own, [state]

    got, nears, queries = [], [], []
    coef, end = scaled, None
    for level in range(levels):
        if level == levels - 1:
            wire = wire[:FIRST]
        bit = 1 << level
        got.append(lax.ppermute(wire, "ctx", [(i, i ^ bit) for i in range(ctx)]))
        if level < 2:
            near, query, *more = near_part(
                asking, gated, mul, coef, skip, flt, end, level * (length // 2), length // 2, block
            )
            coef, end = more if more else (coef, end)
            nears.append(near)
            queries.append(query)
        if level < levels - 1:
            final = level == levels - 2
            wire, *states = join(
                *states, wire, got[level], lam, flt, nears[-1], level, length << level, FIRST if final else ROWS, final
            )
    if levels < 2:
        near, query = near_part(asking, gated, mul, coef, skip, flt, end, length // 2, length // 2, block)
        nears.append(near)
        queries.append(query)

    mixed_out, part = far_part(got, nears, queries, own, asked, mul, coef, lam, skip, flt, out_weight)
    parts = [None, lax.ppermute(part, "chan", [(i, i ^ 1) for i in range(chan)])]
    parts[0] = kept_part(mixed_out, out_weight)
    for stage in range(1, stages):
        send = add_blocks(
            parts, lambda level, i, stage=stage: ((i << (stage + 1)) | (1 << stage)) >> (level + 1), chan >> (stage + 1)
        )
        parts.append(lax.ppermute(send, "chan", [(i, i ^ (1 << stage)) for i in range(chan)]))
    return add_blocks(parts, lambda level, i: 0, 1)[0]


def solution(mesh):
    in_specs = (
        P(None, ("groups", "ctx"), "chan"),
        P(None, None, "chan"),
        P(None, "chan"),
        P(None, "chan"),
        P("chan"),
        P("chan", None),
    )
    out_specs = P(("groups", "ctx"), "chan")
    return jax.shard_map(body, mesh=mesh, in_specs=in_specs, out_specs=out_specs, check_vma=False)
```
